128 devices in a mesh: dp: 16 (over y_hi, x, core), seq: 8 (over z, y_lo).
Axes of the slice: x: 4, y: 4 (y_hi: 2, y_lo: 2; y = y_hi * 2 + y_lo), z: 4, core: 2. Of those that a mesh axis runs over, the one named last changes fastest.
Arguments:
- pre_activation: bfloat16 [16, 32, 128, 512], P('dp', None, 'seq'), may hold values from -6 to 6
- output_grad: bfloat16 [16, 32, 128, 512], P('dp', None, 'seq'), may hold values from -0.59765625 to 0.59765625
- up_kernel: bfloat16 [3, 3, 512, 512], replicated, may hold values from -0.09375 to 0.09375
- in_kernel: bfloat16 [3, 3, 16, 512], replicated, may hold values from -0.09375 to 0.09375
- final_weight: bfloat16 [64, 3072], replicated, may hold values from -0.75 to 0.75
- gate_table: bfloat16 [8, 3072], replicated, may hold values from -4 to 4
- bucket: int32 [16], P('dp'), may hold values from 0 to 7
- query_vectors: bfloat16 [16, 1024, 2048], P('dp', 'seq'), may hold values from -12 to 12
- key_vectors: bfloat16 [16, 1024, 2048], P('dp', 'seq'), may hold values from -12 to 12
- value_vectors: bfloat16 [16, 1024, 2048], P('dp', 'seq'), may hold values from -6 to 6
- out_weight: bfloat16 [2048, 3072], replicated, may hold values from -1.796875 to 1.796875
- block_input: bfloat16 [16, 1024, 3072], P('dp', 'seq'), may hold values from -6 to 6
Outputs:
- query_grad: bfloat16 [16, 1024, 2048], P('dp', 'seq')
- key_grad: bfloat16 [16, 1024, 2048], P('dp', 'seq')
- value_grad: bfloat16 [16, 1024, 2048], P('dp', 'seq')
- weight_grad: float32 [3072, 2048], P(('dp', 'seq'))
The draws below stay inside these ranges and needn't reach their ends.
All inputs are finite; a program needn't handle non-finite values.
Results may differ from the reference program's by a relative error of at most 0.025.
Values may be sent and summed in bfloat16 or wider, within the bound.
No kernel may reach another device: no remote copies, remote signals or barrier semaphores. Data moves between devices by JAX's collectives and lax.ppermute only.
A program may use at most 192 MiB of HBM per device.

```python
import jax
import jax.numpy as jnp
from jax import lax

D = 3072
DH = 128
CH = 512
LAT_CH = 16
HEADS = 16
PW = 64
NB = 8
TOK_DEV = 128
IMG = 16
L = 1024
PH = 16
LAT_H = 32
LAT_W = 128
ATT = 2048
N_SEQ = 8


def attention_pair(key):
    base = jax.random.fold_in(key, 7177)
    streams = jax.random.split(base, 2)
    shape = (IMG, L, HEADS * DH)
    queries = 1.5 * jnp.clip(jax.random.normal(streams[0], shape, jnp.float32), -4.0, 4.0)
    key_rows = 1.5 * jnp.clip(jax.random.normal(streams[1], shape, jnp.float32), -4.0, 4.0)
    return (queries, key_rows)


def draw_query_vectors(key, part):
    return attention_pair(key)[0].astype(jnp.bfloat16)


def draw_key_vectors(key, part):
    return attention_pair(key)[1].astype(jnp.bfloat16)


def touch_ends(drawn, rng, least, high):
    longest = drawn.shape.index(max(drawn.shape))
    spots = []
    for shift in (0, 1):
        where = [jax.random.randint(jax.random.fold_in(rng, axis), (), 0, length) for axis, length in enumerate(drawn.shape)]
        where[longest] = (where[longest] + shift) % drawn.shape[longest]
        spots.append(tuple(where))
    return drawn.at[spots[0]].set(least).at[spots[1]].set(high)


def steps_of(rng, extent, pieces, smallest, largest):
    factor_of, own = 1.0, jax.random.fold_in(rng, 6)
    for axis_at, parts in pieces:
        steps = jnp.exp(jax.random.uniform(jax.random.fold_in(own, axis_at), (parts,), jnp.float32, smallest / len(pieces), largest / len(pieces)))
        factor_of = factor_of * jnp.repeat(steps, extent[axis_at] // parts).reshape([-1 if axis == axis_at else 1 for axis in range(len(extent))])
    return factor_of


def scatter_about(own_key, extent, width, reach, pieces=(), kind=jnp.bfloat16):
    result = jax.random.normal(own_key, extent, jnp.float32) * width
    if len(pieces) > 0:
        result = steps_of(own_key, extent, pieces, -0.22, 0.18) * result
    return jnp.clip(result, min=-reach, max=reach).astype(kind)


def setup_inputs(seed: int = 0) -> dict:
    streams_of = jax.random.split(jax.random.key(seed), 13)
    pre_activation = scatter_about(streams_of[0], (IMG, LAT_H, LAT_W, CH), 1.0, 6.0, ((0, 16), (2, 8)))
    output_grad = scatter_about(streams_of[1], (IMG, LAT_H, LAT_W, CH), 0.1, 0.59765625, ((0, 16), (2, 8)))
    up_kernel = scatter_about(streams_of[2], (3, 3, CH, CH), (9 * CH) ** -0.5, 0.09375)
    in_kernel = scatter_about(streams_of[3], (3, 3, LAT_CH, CH), (9 * CH) ** -0.5, 0.09375)
    final_weight = scatter_about(streams_of[4], (4 * LAT_CH, D), (4 * LAT_CH) ** -0.5, 0.75)
    gate_table = scatter_about(streams_of[5], (NB, D), 1.0, 4.0)
    bucket = touch_ends(jax.random.randint(streams_of[6], (IMG,), 0, NB), jax.random.fold_in(streams_of[6], 1), 0, NB - 1).astype(jnp.int32)
    query_vectors = draw_query_vectors(jax.random.fold_in(streams_of[12], 71), 0)
    key_vectors = draw_key_vectors(jax.random.fold_in(streams_of[12], 71), 0)
    value_vectors = scatter_about(streams_of[9], (IMG, L, ATT), 1.0, 6.0, ((0, 16), (1, 8)))
    out_weight = scatter_about(streams_of[10], (ATT, D), 0.3, 1.796875)
    block_input = scatter_about(streams_of[11], (IMG, L, D), 1.0, 6.0, ((0, 16), (1, 8)))
    return dict(pre_activation=pre_activation, output_grad=output_grad, up_kernel=up_kernel, in_kernel=in_kernel, final_weight=final_weight, gate_table=gate_table, bucket=bucket, query_vectors=query_vectors, key_vectors=key_vectors, value_vectors=value_vectors, out_weight=out_weight, block_input=block_input)


def silu_slope(values):
    sigma = jax.nn.sigmoid(values)
    return sigma * (1.0 + values * (1.0 - sigma))


def transpose_conv(grad, kernel):
    flipped = jnp.transpose(kernel[::-1, ::-1], (0, 1, 3, 2))
    return lax.conv_general_dilated(grad, flipped, (1, 1), ((1, 1), (1, 1)), dimension_numbers=("NHWC", "HWIO", "NHWC"), preferred_element_type=jnp.float32)


def join_heads(stacked):
    return jnp.transpose(stacked, (1, 0, 2)).reshape(stacked.shape[1], stacked.shape[0] * stacked.shape[2])


def reference(pre_activation, output_grad, up_kernel, in_kernel, final_weight, gate_table, bucket, query_vectors, key_vectors, value_vectors, out_weight, block_input):
    softmax_scale = DH ** -0.5

    def one_image(total, inputs):
        feature_pre, cot_image, bucket_id, queries, key_rows, value_rows, input_rows = inputs
        act_grad = transpose_conv(cot_image[None], up_kernel)[0]
        feat_grad = (act_grad * silu_slope(feature_pre.astype(jnp.float32))).astype(jnp.bfloat16)
        latent_grad = transpose_conv(feat_grad[None], in_kernel)[0].astype(jnp.bfloat16)
        patches = latent_grad.reshape(PH, 2, PW, 2, LAT_CH).transpose(0, 2, 1, 3, 4).reshape(L, 4 * LAT_CH)
        stream_grad = jnp.dot(patches, final_weight, preferred_element_type=jnp.float32)
        picker = (jnp.arange(NB, dtype=jnp.int32) == bucket_id).astype(jnp.float32)
        gate_row = jnp.dot(picker, gate_table.astype(jnp.float32), precision=lax.Precision.HIGHEST)
        branch_grad = (stream_grad * gate_row[None, :]).astype(jnp.bfloat16)
        attn_grad = lax.dot_general(branch_grad, out_weight, (((1,), (1,)), ((), ())), preferred_element_type=jnp.float32).astype(jnp.bfloat16)

        def one_head(head):
            start = head * DH
            q_head = lax.dynamic_slice_in_dim(queries, start, DH, 1)
            k_head = lax.dynamic_slice_in_dim(key_rows, start, DH, 1)
            v_head = lax.dynamic_slice_in_dim(value_rows, start, DH, 1)
            g_head = lax.dynamic_slice_in_dim(attn_grad, start, DH, 1)
            scores = lax.dot_general(q_head, k_head, (((1,), (1,)), ((), ())), preferred_element_type=jnp.float32) * softmax_scale
            top = jnp.max(scores, axis=1, keepdims=True)
            weights = jnp.exp(scores - top)
            probs = weights / jnp.sum(weights, axis=1, keepdims=True)
            probs_low = probs.astype(jnp.bfloat16)
            head_out = jnp.dot(probs_low, v_head, preferred_element_type=jnp.float32).astype(jnp.bfloat16)
            row_dot = jnp.sum(g_head.astype(jnp.float32) * head_out.astype(jnp.float32), axis=1, keepdims=True)
            prob_grad = lax.dot_general(g_head, v_head, (((1,), (1,)), ((), ())), preferred_element_type=jnp.float32)
            score_grad = (probs * (prob_grad - row_dot)).astype(jnp.bfloat16)
            q_grad = (jnp.dot(score_grad, k_head, preferred_element_type=jnp.float32) * softmax_scale).astype(jnp.bfloat16)
            logit_tiles = score_grad.reshape(N_SEQ, TOK_DEV, L).astype(jnp.float32)
            query_tiles = q_head.reshape(N_SEQ, TOK_DEV, DH).astype(jnp.float32)
            key_portion = (jnp.einsum("jnp,jnt->jpt", logit_tiles, query_tiles) * softmax_scale).astype(jnp.bfloat16)
            probability_tiles = probs_low.reshape(N_SEQ, TOK_DEV, L).astype(jnp.float32)
            gradient_tiles = g_head.reshape(N_SEQ, TOK_DEV, DH).astype(jnp.float32)
            value_portion = jnp.einsum("jnp,jnt->jpt", probability_tiles, gradient_tiles).astype(jnp.bfloat16)
            k_grad = jnp.sum(key_portion.astype(jnp.float32), axis=0).astype(jnp.bfloat16)
            v_grad = jnp.sum(value_portion.astype(jnp.float32), axis=0).astype(jnp.bfloat16)
            return q_grad, k_grad, v_grad

        q_all, k_all, v_all = lax.map(one_head, jnp.arange(HEADS, dtype=jnp.int32))
        value_joined = join_heads(v_all)
        term = lax.dot_general(input_rows, value_joined, (((0,), (0,)), ((), ())), preferred_element_type=jnp.float32)
        return total + term, (join_heads(q_all), join_heads(k_all), value_joined)

    start_total = jnp.zeros((D, ATT), jnp.float32)
    weight_grad, grads = lax.scan(one_image, start_total, (pre_activation, output_grad, bucket, query_vectors, key_vectors, value_vectors, block_input))
    return grads[0], grads[1], grads[2], weight_grad
```

```python
import functools
import math

import jax
import jax.numpy as jnp
from jax import lax
from jax.experimental import pallas as pl
from jax.experimental.pallas import tpu as pltpu
from jax.sharding import PartitionSpec as P

DH = 128
SCALE = DH ** (-0.5)


def with_halo(block, sides, width):
    for axis, dim in sides:
        count = lax.axis_size(axis)
        forward = [(i, i + 1) for i in range(count - 1)]
        backward = [(target, source) for source, target in forward]
        low = lax.ppermute(
            lax.slice_in_dim(block, block.shape[dim] - width, None, axis=dim), axis, forward
        )
        high = lax.ppermute(lax.slice_in_dim(block, 0, width, axis=dim), axis, backward)
        block = jnp.concatenate([low, block, high], axis=dim)
    return block


def silu_slope(values):
    sigma = jax.nn.sigmoid(values)
    return sigma * (1.0 + values * (1.0 - sigma))


def column_grad(grad, kernel):
    widened = with_halo(grad, (("seq", 2),), 1)
    flipped = jnp.transpose(kernel[::-1, ::-1], (0, 1, 3, 2))
    return lax.conv_general_dilated(
        widened,
        flipped,
        (1, 1),
        ((1, 1), (0, 0)),
        dimension_numbers=("NHWC", "HWIO", "NHWC"),
        preferred_element_type=jnp.float32,
    )


def dot(a, b, ca, cb):
    return lax.dot_general(a, b, (((ca,), (cb,)), ((), ())), preferred_element_type=jnp.float32)


def attention_kernel(q_ref, k_ref, v_ref, pat_ref, mix_ref, qg_ref, kg_ref, vg_ref, kt_ref, kacc, vacc):
    tile = pl.program_id(1)

    @pl.when(tile == 0)
    def _():
        kt_ref[...] = k_ref[...].T
        kacc[...] = jnp.zeros_like(kacc)
        vacc[...] = jnp.zeros_like(vacc)

    q = q_ref[...]
    grad_t = dot(mix_ref[...], pat_ref[...], 0, 1)
    scores = dot(k_ref[...], q, 1, 1)
    top = jnp.max(scores, axis=0, keepdims=True)
    step = SCALE * math.log2(math.e)
    weights = jnp.exp2(scores * step - top * step)
    inverse = 1.0 / jnp.sum(weights, axis=0, keepdims=True)
    grad_low = (grad_t * inverse).astype(jnp.bfloat16)
    prob_grad = dot(v_ref[...], grad_low, 1, 0)
    row_dot = jnp.sum(weights * prob_grad, axis=0, keepdims=True) * inverse
    score_grad = (weights * (prob_grad - row_dot)).astype(jnp.bfloat16)
    vacc[...] += dot(weights.astype(jnp.bfloat16), grad_low, 1, 1)
    kacc[...] += dot(score_grad, q, 1, 0)
    qg_ref[...] = (dot(kt_ref[...], score_grad, 1, 0).T * SCALE).astype(jnp.bfloat16)

    @pl.when(tile == pl.num_programs(1) - 1)
    def _():
        kg_ref[...] = (kacc[...] * SCALE).astype(jnp.bfloat16)
        vg_ref[...] = vacc[...].astype(jnp.bfloat16)


def attention(qkv, patches, mix):
    tokens = qkv.shape[0]
    heads = qkv.shape[1] // (3 * DH)
    tile = 512
    out = jax.ShapeDtypeStruct((tokens, heads * DH), jnp.bfloat16)
    return pl.pallas_call(
        attention_kernel,
        grid=(heads, tokens // tile),
        in_specs=[
            pl.BlockSpec((tile, DH), lambda h, t: (t, h)),
            pl.BlockSpec((tokens, DH), lambda h, t: (0, heads + h)),
            pl.BlockSpec((tokens, DH), lambda h, t: (0, 2 * heads + h)),
            pl.BlockSpec((tile, patches.shape[1]), lambda h, t: (t, 0)),
            pl.BlockSpec((mix.shape[0], DH), lambda h, t: (0, h)),
        ],
        out_specs=[
            pl.BlockSpec((tile, DH), lambda h, t: (t, h)),
            pl.BlockSpec((tokens, DH), lambda h, t: (0, h)),
            pl.BlockSpec((tokens, DH), lambda h, t: (0, h)),
        ],
        out_shape=[out, out, out],
        scratch_shapes=[
            pltpu.VMEM((DH, tokens), jnp.bfloat16),
            pltpu.VMEM((tokens, DH), jnp.float32),
            pltpu.VMEM((tokens, DH), jnp.float32),
        ],
        compiler_params=pltpu.CompilerParams(vmem_limit_bytes=48 * 1024 * 1024),
        cost_estimate=pl.CostEstimate(
            flops=5 * 2 * heads * tokens * tokens * DH,
            bytes_accessed=6 * tokens * heads * DH * 2,
            transcendentals=heads * tokens * tokens,
        ),
        name="attention",
    )(qkv, qkv, qkv, patches, mix)


def per_device(
    pre_activation,
    output_grad,
    up_kernel,
    in_kernel,
    final_weight,
    gate_table,
    bucket,
    query_vectors,
    key_vectors,
    value_vectors,
    out_weight,
    block_input,
):
    seq_size = lax.axis_size("seq")
    me_seq = lax.axis_index("seq")
    me_dp = lax.axis_index("dp")
    zed, low = me_seq // 2, me_seq % 2
    core, ex = me_dp % 2, (me_dp // 2) % 4
    tokens, width = query_vectors.shape[1:]
    cols = width // seq_size

    def seq_move(x, target):
        return lax.ppermute(x, "seq", [(i, target(i)) for i in range(8)])

    def dp_move(x, target):
        return lax.ppermute(x, "dp", [(i, target(i)) for i in range(16)])

    act_grad = column_grad(output_grad, up_kernel)

    by_owner = jnp.concatenate(
        [
            x[0].reshape(tokens, seq_size, cols)
            for x in (query_vectors, key_vectors, value_vectors)
        ],
        axis=2,
    ).transpose(1, 0, 2)
    qkv = lax.all_to_all(by_owner, "seq", 0, 0, tiled=True).reshape(seq_size * tokens, 3 * cols)

    rows = block_input[0]
    half = rows.shape[1] // 2
    kept = lax.dynamic_slice_in_dim(rows, low * half, half, 1)
    given = lax.dynamic_slice_in_dim(rows, (1 - low) * half, half, 1)
    got = seq_move(given, lambda i: i ^ 1)
    pair = jnp.where(
        low == 0, jnp.concatenate([kept, got], 0), jnp.concatenate([got, kept], 0)
    )
    left = seq_move(pair, lambda i: (i + 2) % 8)
    right = seq_move(pair, lambda i: (i - 2) % 8)
    far_a = seq_move(left[:tokens], lambda i: (i + 2) % 8)
    far_b = seq_move(right[tokens:], lambda i: (i - 2) % 8)
    rows_all = jnp.concatenate([pair, left, right, far_a, far_b], 0)

    gate_row = lax.dynamic_slice_in_dim(gate_table, bucket[0], 1, 0)
    gated = final_weight.astype(jnp.float32) * gate_row.astype(jnp.float32)
    gated_high = gated.astype(jnp.bfloat16)
    gated_rest = (gated - gated_high.astype(jnp.float32)).astype(jnp.bfloat16)
    out_part = lax.dynamic_slice_in_dim(out_weight, me_seq * cols, cols, 0)
    mixes = dot(jnp.concatenate([gated_high, gated_rest], 0), out_part, 1, 1)
    mix = mixes[: mixes.shape[0] // 2] + mixes[mixes.shape[0] // 2 :]
    mix_high = mix.astype(jnp.bfloat16)
    mix_rest = (mix - mix_high.astype(jnp.float32)).astype(jnp.bfloat16)
    mix = jnp.concatenate([mix_high, mix_rest], 0)

    feat_grad = (act_grad * silu_slope(pre_activation.astype(jnp.float32))).astype(jnp.bfloat16)
    latent_grad = column_grad(feat_grad, in_kernel).astype(jnp.bfloat16)
    lat_rows, lat_cols, chans = latent_grad.shape[1:]
    strip = (
        latent_grad.reshape(lat_rows // 2, 2, lat_cols // 2, 2, chans)
        .transpose(0, 2, 1, 3, 4)
        .reshape(lat_rows // 2, lat_cols // 2, 4 * chans)
    )
    strip = jnp.concatenate([strip, strip], 2)
    strips = lax.all_to_all(
        jnp.broadcast_to(strip[None], (seq_size,) + strip.shape), "seq", 0, 0, tiled=True
    )
    patches = strips.transpose(1, 0, 2, 3).reshape(seq_size * tokens, 8 * chans)

    q_part, k_part, v_part = attention(qkv, patches, mix)

    v_got = seq_move(v_part, lambda i: i ^ 1)
    v_pair = jnp.where(
        low == 0, jnp.concatenate([v_part, v_got], 1), jnp.concatenate([v_got, v_part], 1)
    ).reshape(4, 2 * tokens, 2 * cols)
    v_all = jnp.concatenate(
        [lax.dynamic_index_in_dim(v_pair, (zed + d) % 4, 0, False) for d in (0, 3, 1, 2)], 0
    )
    term = dot(rows_all, v_all, 0, 0)

    wide = term.shape[1]
    block = term.shape[0] // 8
    term = term.reshape(4, 2, block, wide)
    mine = lax.dynamic_index_in_dim(term, core, 1, False)
    other = lax.dynamic_index_in_dim(term, 1 - core, 1, False).astype(jnp.bfloat16)
    mine = mine + dp_move(other, lambda i: i ^ 1).astype(jnp.float32)
    low_mine = mine.astype(jnp.bfloat16)
    total = lax.dynamic_index_in_dim(mine, ex, 0, False)
    for d in (1, 2, 3):
        piece = lax.dynamic_index_in_dim(low_mine, ex ^ d, 0, False)
        total = total + dp_move(piece, lambda i, d=d: i ^ (2 * d)).astype(jnp.float32)
    total = total.astype(jnp.bfloat16).reshape(4, 2, block // 8, wide)

    high = me_dp // 8
    result = jnp.zeros((4, block // 8, wide), jnp.float32)
    for d in range(4):
        landed = 0.0
        for b in range(2):
            perm = []
            for dp in range(16):
                for s in range(8):
                    yh, xc, z, yl = dp // 8, dp % 8, s // 2, s % 2
                    perm.append((dp * 8 + s, (yl * 8 + xc) * 8 + ((z + d) % 4) * 2 + (yh ^ b)))
            piece = lax.dynamic_slice(
                total, ((zed + d) % 4, high ^ b, 0, 0), (1, 1) + total.shape[2:]
            )[0, 0]
            landed = landed + lax.ppermute(piece, ("dp", "seq"), perm).astype(jnp.float32)
        result = lax.dynamic_update_slice(result, landed[None], ((zed - d) % 4, 0, 0))
    weight_grad = result.transpose(1, 0, 2).reshape(block // 8, 4 * wide)

    def spread(part):
        blocks = lax.all_to_all(
            part.reshape(seq_size, tokens, cols), "seq", 0, 0, tiled=True
        )
        return blocks.transpose(1, 0, 2).reshape(1, tokens, width)

    return (spread(q_part), spread(k_part), spread(v_part), weight_grad)


def solution(mesh):
    return jax.shard_map(
        per_device,
        mesh=mesh,
        in_specs=(
            P("dp", None, "seq", None),
            P("dp", None, "seq", None),
            P(),
            P(),
            P(),
            P(),
            P("dp"),
            P("dp", "seq", None),
            P("dp", "seq", None),
            P("dp", "seq", None),
            P(),
            P("dp", "seq", None),
        ),
        out_specs=(
            P("dp", "seq", None),
            P("dp", "seq", None),
            P("dp", "seq", None),
            P(("dp", "seq"), None),
        ),
        check_vma=False,
    )
```

```python
import functools
import math

import jax
import jax.numpy as jnp
from jax import lax
from jax.experimental import pallas as pl
from jax.experimental.pallas import tpu as pltpu
from jax.sharding import PartitionSpec as P

DH = 128
SCALE = DH ** (-0.5)


def dot(a, b, ca, cb):
    return lax.dot_general(a, b, (((ca,), (cb,)), ((), ())), preferred_element_type=jnp.float32)


def roll(x, shift, axis):
    return pltpu.roll(x, shift % x.shape[axis], axis)


def conv_kernel(grad_ref, low_ref, high_ref, up_ref, pre_ref, in_ref, out_ref, shifted, acc, feat, taps, lat):
    step = pl.program_id(0)
    rows, cols, chans = grad_ref.shape
    pixels = rows * cols

    @pl.when(step == 0)
    def _():
        grad = grad_ref[...].astype(jnp.float32)
        at = lax.broadcasted_iota(jnp.int32, grad.shape, 1)
        left = jnp.where(at == 0, low_ref[...].astype(jnp.float32), roll(grad, 1, 1))
        right = jnp.where(at == cols - 1, high_ref[...].astype(jnp.float32), roll(grad, -1, 1))
        zero = jnp.zeros((cols, chans), jnp.bfloat16)
        for i, x in enumerate((left, grad, right)):
            shifted[i, :cols] = zero
            shifted[i, cols + pixels :] = zero
            shifted[i, cols : cols + pixels] = x.astype(jnp.bfloat16).reshape(pixels, chans)
        acc[...] = jnp.zeros_like(acc)
        feat[:cols] = zero
        feat[cols + pixels :] = zero
        taps[...] = jnp.zeros_like(taps)
        taps[:, : in_ref.shape[1]] = in_ref[...]

    start = pl.multiple_of((step // 3) * cols, cols)
    acc[...] += dot(shifted[step % 3, pl.ds(start, pixels)], up_ref[0, 0], 1, 1)

    @pl.when(step == 8)
    def _():
        pre = pre_ref[...].astype(jnp.float32)
        sigma = jax.nn.sigmoid(pre)
        slope = sigma * (1.0 + pre * (1.0 - sigma))
        feat[cols : cols + pixels] = (acc[...] * slope).astype(jnp.bfloat16)
        part = sum(dot(feat[a * cols : a * cols + pixels], taps[2 - a], 1, 1) for a in range(3))
        part = part.reshape(rows, cols, 128)
        lane = lax.broadcasted_iota(jnp.int32, part.shape, 2)
        at = lax.broadcasted_iota(jnp.int32, part.shape, 1)
        after = jnp.where(lane < 16, part, 0.0)
        here = jnp.where(lane < 16, roll(part, -16, 2), 0.0)
        before = jnp.where(lane < 16, roll(part, -32, 2), 0.0)
        inner = (
            here
            + jnp.where(at == 0, 0.0, roll(before, 1, 1))
            + jnp.where(at == cols - 1, 0.0, roll(after, -1, 1))
        )
        edge = jnp.where(at == 0, roll(before, 1, 1), 0.0) + jnp.where(
            at == cols - 1, roll(after, -1, 1), 0.0
        )
        lat[...] = (inner + roll(edge, 64, 2)).reshape(pixels, 128)
        total = 0.0
        for b in range(2):
            pick = lat[pl.ds(b, pixels // 2, stride=2), :]
            pick = pick.reshape(rows // 2, 2, cols // 2, 128)
            for a in range(2):
                total = total + roll(pick[:, a], (2 * a + b) * 16, 2)
        out_ref[...] = total.reshape(pixels // 4, 128).astype(jnp.bfloat16)


def decoder(grad, low, high, up_kernel, pre, in_kernel):
    rows, cols, chans = grad.shape
    pixels = rows * cols
    taps = in_kernel.reshape(3, -1, chans)
    whole = lambda *shape: pl.BlockSpec(shape, lambda t: (0,) * len(shape))
    return pl.pallas_call(
        conv_kernel,
        grid=(9,),
        in_specs=[
            whole(rows, cols, chans),
            whole(rows, 1, chans),
            whole(rows, 1, chans),
            pl.BlockSpec((1, 1, chans, chans), lambda t: (2 - t // 3, 2 - t % 3, 0, 0)),
            whole(pixels, chans),
            whole(*taps.shape),
        ],
        out_specs=whole(pixels // 4, 128),
        out_shape=jax.ShapeDtypeStruct((pixels // 4, 128), jnp.bfloat16),
        scratch_shapes=[
            pltpu.VMEM((3, pixels + 2 * cols, chans), jnp.bfloat16),
            pltpu.VMEM((pixels, chans), jnp.float32),
            pltpu.VMEM((pixels + 2 * cols, chans), jnp.bfloat16),
            pltpu.VMEM((3, 128, chans), jnp.bfloat16),
            pltpu.VMEM((pixels, 128), jnp.float32),
        ],
        compiler_params=pltpu.CompilerParams(vmem_limit_bytes=32 * 1024 * 1024),
        cost_estimate=pl.CostEstimate(
            flops=2 * 9 * pixels * chans * chans, bytes_accessed=9 * chans * chans * 2,
            transcendentals=pixels * chans,
        ),
        name="decoder",
    )(grad, low, high, up_kernel, pre.reshape(pixels, chans), taps)


def value_kernel(
    seat, q_ref, k_ref, own_ref, mate_ref, near_ref, far_ref, last_ref, mix_ref,
    e_ref, g_ref, inv_ref, vg_ref, strips, patches, vacc,
):
    head, tile = pl.program_id(0), pl.program_id(1)
    me = seat[0]

    @pl.when((head == 0) & (tile == 0))
    def _():
        strips[0] = jnp.zeros(strips.shape[1:], jnp.float32)
        strips[9] = jnp.zeros(strips.shape[1:], jnp.float32)
        strips[me + 1] = own_ref[...].astype(jnp.float32)
        strips[(me ^ 1) + 1] = mate_ref[...].astype(jnp.float32)
        for d, ref in ((2, near_ref), (4, far_ref), (6, last_ref)):
            for b in range(2):
                strips[(me ^ d ^ b) + 1] = ref[b].astype(jnp.float32)
        shape = (16, 8, 128)
        at = lax.broadcasted_iota(jnp.int32, shape, 1)
        lane = lax.broadcasted_iota(jnp.int32, shape, 2)
        for s in range(8):
            mine = strips[s + 1].reshape(shape)
            below = roll(strips[s].reshape(shape), 64, 2)
            above = roll(strips[s + 2].reshape(shape), 64, 2)
            joined = mine + jnp.where((at == 0) & (lane % 32 < 16), below, 0.0)
            joined = joined + jnp.where((at == 7) & (lane % 32 >= 16), above, 0.0)
            joined = jnp.where(lane < 64, joined, 0.0)
            patches[:, s * 8 : s * 8 + 8, :] = joined + roll(joined, 64, 2)

    @pl.when(tile == 0)
    def _():
        vacc[...] = jnp.zeros_like(vacc)

    size = q_ref.shape[0]
    q = q_ref[...]
    group = size // 64
    pat = patches[pl.ds(tile * group, group)].reshape(size, 128).astype(jnp.bfloat16)
    grad_t = dot(mix_ref[...], pat, 0, 1)
    scores = dot(k_ref[...], q, 1, 1)
    top = jnp.max(scores, axis=0, keepdims=True)
    scale = SCALE * math.log2(math.e)
    weights = jnp.exp2(scores * scale - top * scale)
    inverse = 1.0 / jnp.sum(weights, axis=0, keepdims=True)
    grad_low = (grad_t * inverse).astype(jnp.bfloat16)
    low = weights.astype(jnp.bfloat16)
    e_ref[0] = low
    g_ref[0] = grad_low
    inv_ref[0] = inverse
    vacc[...] += dot(low, grad_low, 1, 1)

    @pl.when(tile == pl.num_programs(1) - 1)
    def _():
        vg_ref[...] = vacc[...].astype(jnp.bfloat16)


def value_part(qk, strips, mix, me, tile=512):
    tokens = qk.shape[0]
    heads = qk.shape[1] // (2 * DH)
    own, mate, near, far, last = strips
    whole = lambda x: pl.BlockSpec(x.shape, lambda h, t, s: (0,) * x.ndim)
    return pl.pallas_call(
        value_kernel,
        grid_spec=pltpu.PrefetchScalarGridSpec(
            num_scalar_prefetch=1,
            grid=(heads, tokens // tile),
            in_specs=[
                pl.BlockSpec((tile, DH), lambda h, t, s: (t, h)),
                pl.BlockSpec((tokens, DH), lambda h, t, s: (0, heads + h)),
                whole(own),
                whole(mate),
                whole(near),
                whole(far),
                whole(last),
                pl.BlockSpec((mix.shape[0], DH), lambda h, t, s: (0, h)),
            ],
            out_specs=[
                pl.BlockSpec((1, tokens, tile), lambda h, t, s: (h, 0, t)),
                pl.BlockSpec((1, DH, tile), lambda h, t, s: (h, 0, t)),
                pl.BlockSpec((1, 1, tile), lambda h, t, s: (h, 0, t)),
                pl.BlockSpec((tokens, DH), lambda h, t, s: (0, h)),
            ],
            scratch_shapes=[
                pltpu.VMEM((10, 128, 128), jnp.float32),
                pltpu.VMEM((16, 64, 128), jnp.float32),
                pltpu.VMEM((tokens, DH), jnp.float32),
            ],
        ),
        out_shape=[
            jax.ShapeDtypeStruct((heads, tokens, tokens), jnp.bfloat16),
            jax.ShapeDtypeStruct((heads, DH, tokens), jnp.bfloat16),
            jax.ShapeDtypeStruct((heads, 1, tokens), jnp.float32),
            jax.ShapeDtypeStruct((tokens, heads * DH), jnp.bfloat16),
        ],
        compiler_params=pltpu.CompilerParams(vmem_limit_bytes=40 * 1024 * 1024),
        cost_estimate=pl.CostEstimate(
            flops=2 * 2 * heads * tokens * tokens * DH,
            bytes_accessed=heads * tokens * tokens * 2,
            transcendentals=heads * tokens * tokens,
        ),
        name="value_part",
    )(me[None], qk, qk, own, mate, near, far, last, mix)


def score_kernel(q_ref, k_ref, v_ref, e_ref, g_ref, inv_ref, out_ref, kt_ref, kacc):
    head, tile = pl.program_id(0), pl.program_id(1)
    heads = pl.num_programs(0)

    @pl.when(tile == 0)
    def _():
        kt_ref[...] = k_ref[...].T
        kacc[...] = jnp.zeros_like(kacc)

    size = q_ref.shape[0]
    q = q_ref[...]
    weights = e_ref[0].astype(jnp.float32)
    prob_grad = dot(v_ref[...], g_ref[0], 1, 0)
    row_dot = jnp.sum(weights * prob_grad, axis=0, keepdims=True) * inv_ref[0]
    score_grad = (weights * (prob_grad - row_dot)).astype(jnp.bfloat16)
    kacc[...] += dot(score_grad, q, 1, 0)
    rows = pl.ds(pl.multiple_of(tile * size, size), size)
    at = pl.ds(pl.multiple_of(head * DH, DH), DH)
    out_ref[rows, at] = (dot(kt_ref[...], score_grad, 1, 0).T * SCALE).astype(jnp.bfloat16)

    @pl.when(tile == pl.num_programs(1) - 1)
    def _():
        at = pl.ds(pl.multiple_of((heads + head) * DH, DH), DH)
        out_ref[:, at] = (kacc[...] * SCALE).astype(jnp.bfloat16)


def score_part(qk, v, e, g, inv, tile=512):
    tokens = qk.shape[0]
    heads = qk.shape[1] // (2 * DH)
    return pl.pallas_call(
        score_kernel,
        grid=(heads, tokens // tile),
        in_specs=[
            pl.BlockSpec((tile, DH), lambda h, t: (t, h)),
            pl.BlockSpec((tokens, DH), lambda h, t: (0, heads + h)),
            pl.BlockSpec((tokens, DH), lambda h, t: (0, h)),
            pl.BlockSpec((1, tokens, tile), lambda h, t: (h, 0, t)),
            pl.BlockSpec((1, DH, tile), lambda h, t: (h, 0, t)),
            pl.BlockSpec((1, 1, tile), lambda h, t: (h, 0, t)),
        ],
        out_specs=pl.BlockSpec((tokens, 2 * heads * DH), lambda h, t: (0, 0)),
        out_shape=jax.ShapeDtypeStruct((tokens, 2 * heads * DH), jnp.bfloat16),
        scratch_shapes=[
            pltpu.VMEM((DH, tokens), jnp.bfloat16),
            pltpu.VMEM((tokens, DH), jnp.float32),
        ],
        compiler_params=pltpu.CompilerParams(vmem_limit_bytes=40 * 1024 * 1024),
        cost_estimate=pl.CostEstimate(
            flops=3 * 2 * heads * tokens * tokens * DH,
            bytes_accessed=heads * tokens * tokens * 2,
            transcendentals=0,
        ),
        name="score_part",
    )(qk, qk, v, e, g, inv)


def weight_kernel(seat, pair, left, right, far_a, far_b, v_own, v_got, mine_ref, other_ref, acc):
    zed, low, core = seat[0], seat[1], seat[2]
    first = pl.multiple_of(low * 128, 128)
    second = pl.multiple_of((1 - low) * 128, 128)
    total = 0.0
    for d, ref in ((0, pair), (3, left), (1, right), (2, None)):
        at = pl.multiple_of(((zed + d) % 4) * 256, 256)
        if ref is None:
            a, b = far_a[...], far_b[...]
            top = jnp.where(low == 0, a, b)
            end = jnp.where(low == 0, b, a)
        else:
            top, end = ref[pl.ds(first, 128)], ref[pl.ds(second, 128)]
        rows = jnp.concatenate([top, end], 0)
        v = jnp.concatenate([v_own[pl.ds(at, 256)], v_got[pl.ds(at, 256)]], 1)
        total = total + dot(rows, v, 0, 0)
    acc[...] = total
    block = total.shape[0] // 2
    mine_ref[0] = acc[pl.ds(pl.multiple_of(core * block, 8), block)]
    other_ref[0] = acc[pl.ds(pl.multiple_of((1 - core) * block, 8), block)].astype(jnp.bfloat16)


def weight_part(pieces, v_own, v_got, seat):
    half = pieces[0].shape[1]
    step = half // 4
    cols = 2 * v_own.shape[1]
    whole = lambda x: pl.BlockSpec(x.shape, lambda i, s: (0,) * x.ndim)
    out = pl.BlockSpec((1, step // 2, cols), lambda i, s: (i, 0, 0))
    return pl.pallas_call(
        weight_kernel,
        grid_spec=pltpu.PrefetchScalarGridSpec(
            num_scalar_prefetch=1,
            grid=(4,),
            in_specs=[pl.BlockSpec((x.shape[0], step), lambda i, s: (0, i)) for x in pieces]
            + [whole(v_own), whole(v_got)],
            out_specs=[out, out],
            scratch_shapes=[pltpu.VMEM((step, cols), jnp.float32)],
        ),
        out_shape=[
            jax.ShapeDtypeStruct((4, step // 2, cols), jnp.float32),
            jax.ShapeDtypeStruct((4, step // 2, cols), jnp.bfloat16),
        ],
        compiler_params=pltpu.CompilerParams(vmem_limit_bytes=32 * 1024 * 1024),
        cost_estimate=pl.CostEstimate(
            flops=2 * 1024 * half * cols, bytes_accessed=1024 * half * 2, transcendentals=0
        ),
        name="weight_part",
    )(seat, *pieces, v_own, v_got)


def place_kernel(seat, own, one, two, three, out_ref):
    zed, high = seat[0], seat[1]
    cols = own.shape[1] // 2
    for d, ref in enumerate((own, one, two, three)):
        source = (zed + 4 - d) % 4
        for h in range(2):
            at = pl.multiple_of((source * 2 + (high ^ h)) * cols, cols)
            out_ref[:, pl.ds(at, cols)] = ref[:, h * cols : (h + 1) * cols]


def place(parts, seat):
    rows, cols = parts[0].shape
    whole = pl.BlockSpec((rows, cols), lambda i, s: (0, 0))
    return pl.pallas_call(
        place_kernel,
        grid_spec=pltpu.PrefetchScalarGridSpec(
            num_scalar_prefetch=1,
            grid=(1,),
            in_specs=[whole] * 4,
            out_specs=pl.BlockSpec((rows, 4 * cols), lambda i, s: (0, 0)),
        ),
        out_shape=jax.ShapeDtypeStruct((rows, 4 * cols), jnp.float32),
        name="place",
    )(seat, *parts)


def per_device(
    pre_activation,
    output_grad,
    up_kernel,
    in_kernel,
    final_weight,
    gate_table,
    bucket,
    query_vectors,
    key_vectors,
    value_vectors,
    out_weight,
    block_input,
):
    seq_size = lax.axis_size("seq")
    me_seq = lax.axis_index("seq")
    me_dp = lax.axis_index("dp")
    zed, low = me_seq // 2, me_seq % 2
    core, ex, high = me_dp % 2, (me_dp // 2) % 4, me_dp // 8
    tokens, width = query_vectors.shape[1:]
    cols = width // seq_size

    def seq_move(x, target):
        return lax.ppermute(x, "seq", [(i, target(i)) for i in range(8)])

    def dp_move(x, target):
        return lax.ppermute(x, "dp", [(i, target(i)) for i in range(16)])

    grad = output_grad[0]
    forward = [(i, i + 1) for i in range(seq_size - 1)]
    backward = [(i + 1, i) for i in range(seq_size - 1)]
    from_low = lax.ppermute(grad[:, -1:], "seq", forward)
    from_high = lax.ppermute(grad[:, :1], "seq", backward)

    def gather_tokens(*arrays):
        split = jnp.concatenate([x[0].reshape(tokens, seq_size, cols) for x in arrays], axis=2)
        moved = lax.all_to_all(split.transpose(1, 0, 2), "seq", 0, 0, tiled=True)
        return moved.reshape(seq_size * tokens, len(arrays) * cols)

    qk = gather_tokens(query_vectors, key_vectors)
    values = gather_tokens(value_vectors)

    rows = block_input[0]
    half = rows.shape[1] // 2
    kept = lax.dynamic_slice_in_dim(rows, low * half, half, 1)
    given = lax.dynamic_slice_in_dim(rows, (1 - low) * half, half, 1)
    pair = jnp.concatenate([kept, seq_move(given, lambda i: i ^ 1)], 0)
    left = seq_move(pair, lambda i: (i + 2) % 8)
    right = seq_move(pair, lambda i: (i - 2) % 8)
    far_a = seq_move(left[:tokens], lambda i: (i + 2) % 8)
    far_b = seq_move(right[tokens:], lambda i: (i - 2) % 8)

    gate_row = lax.dynamic_slice_in_dim(gate_table, bucket[0], 1, 0)
    gated = final_weight.astype(jnp.float32) * gate_row.astype(jnp.float32)
    gated_high = gated.astype(jnp.bfloat16)
    gated_rest = (gated - gated_high.astype(jnp.float32)).astype(jnp.bfloat16)
    out_part = lax.dynamic_slice_in_dim(out_weight, me_seq * cols, cols, 0)
    mixes = dot(jnp.concatenate([gated_high, gated_rest], 0), out_part, 1, 1)
    mix = mixes[: mixes.shape[0] // 2] + mixes[mixes.shape[0] // 2 :]
    mix_high = mix.astype(jnp.bfloat16)
    mix_rest = (mix - mix_high.astype(jnp.float32)).astype(jnp.bfloat16)
    mix = jnp.concatenate([mix_high, mix_rest], 0)

    strip = decoder(grad, from_low, from_high, up_kernel, pre_activation[0], in_kernel)
    mate = seq_move(strip, lambda i: i ^ 1)
    both = jnp.stack([strip, mate])
    others = [seq_move(both, lambda i, d=d: i ^ d) for d in (2, 4, 6)]

    e, g, inv, v_part = value_part(qk, (strip, mate, *others), mix, me_seq)
    v_got = seq_move(v_part, lambda i: i ^ 1)
    qk_part = score_part(qk, values, e, g, inv)

    mine, other = weight_part(
        (pair, left, right, far_a, far_b), v_part, v_got, jnp.stack([zed, low, core])
    )
    mine = mine + dp_move(other, lambda i: i ^ 1).astype(jnp.float32)
    low_mine = mine.astype(jnp.bfloat16)
    total = lax.dynamic_index_in_dim(mine, ex, 0, False)
    for d in (1, 2, 3):
        piece = lax.dynamic_index_in_dim(low_mine, ex ^ d, 0, False)
        total = total + dp_move(piece, lambda i, d=d: i ^ (2 * d)).astype(jnp.float32)
    wide = total.shape[1]
    total = total.astype(jnp.bfloat16).reshape(4, 2, -1, wide)

    landed = 0.0
    for b in range(2):
        perm = []
        for dp in range(16):
            for s in range(8):
                yh, xc, z, yl = dp // 8, dp % 8, s // 2, s % 2
                perm.append((dp * 8 + s, (yl * 8 + xc) * 8 + z * 2 + (yh ^ b)))
        piece = lax.dynamic_index_in_dim(total, high ^ b, 1, False)
        landed = landed + lax.ppermute(piece, ("dp", "seq"), perm).astype(jnp.float32)
    parts = [lax.dynamic_index_in_dim(landed, zed, 0, False)]
    for d in (1, 2, 3):
        piece = lax.dynamic_index_in_dim(landed, (zed + d) % 4, 0, False)
        parts.append(seq_move(piece, lambda i, d=d: (i + 2 * d) % 8))
    weight_grad = place(parts, jnp.stack([zed, high]))

    def spread(part):
        return lax.all_to_all(part.reshape(seq_size, tokens, -1), "seq", 0, 0, tiled=True)

    def tokens_of(blocks):
        return blocks.transpose(1, 0, 2).reshape(1, tokens, width)

    value_grad = tokens_of(spread(v_part))
    qk_out = spread(qk_part)
    return (tokens_of(qk_out[:, :, :cols]), tokens_of(qk_out[:, :, cols:]), value_grad, weight_grad)


def solution(mesh):
    return jax.shard_map(
        per_device,
        mesh=mesh,
        in_specs=(
            P("dp", None, "seq", None),
            P("dp", None, "seq", None),
            P(),
            P(),
            P(),
            P(),
            P("dp"),
            P("dp", "seq", None),
            P("dp", "seq", None),
            P("dp", "seq", None),
            P(),
            P("dp", "seq", None),
        ),
        out_specs=(
            P("dp", "seq", None),
            P("dp", "seq", None),
            P("dp", "seq", None),
            P(("dp", "seq"), None),
        ),
        check_vma=False,
    )
```

```python
import math

import jax
import jax.numpy as jnp
from jax import lax
from jax.experimental import pallas as pl
from jax.experimental.pallas import tpu as pltpu
from jax.sharding import PartitionSpec as P


DH = 128
SCALE = DH ** (-0.5)
CHUNK = 512
PART = 512
SLAB = 128


def dot(a, b, ca, cb):
    return lax.dot_general(a, b, (((ca,), (cb,)), ((), ())), preferred_element_type=jnp.float32)


def roll(x, shift, axis):
    return pltpu.roll(x, shift % x.shape[axis], axis)


def after(x, first):
    return lax.optimization_barrier((x, first))[0]


def conv_kernel(
    seat, bucket, grad_ref, low_ref, high_ref, up_ref, pre_ref, in_ref, table_ref, final_ref,
    weight_ref, out_ref, mix_ref, shifted, feat, taps, lat, ups, part_ref, sems,
):
    rows, cols, chans = grad_ref.shape
    pixels = rows * cols

    copies = [
        pltpu.make_async_copy(up_ref.at[2 - a, 2 - b], ups.at[3 * a + b], sems.at[3 * a + b])
        for a in range(3)
        for b in range(3)
    ]
    early = copies[1::3] + copies[0::3] + copies[2::3]
    count = part_ref.shape[0]
    first = pl.multiple_of(seat[0] * count, count)
    copies.append(
        pltpu.make_async_copy(weight_ref.at[pl.ds(first, count)], part_ref, sems.at[9])
    )
    for copy in early + copies[9:]:
        copy.start()
    zero = jnp.zeros((cols, chans), jnp.bfloat16)
    feat[:cols] = zero
    feat[cols + pixels :] = zero
    taps[...] = jnp.zeros_like(taps)
    taps[:, : in_ref.shape[1]] = in_ref[...]
    at = lax.broadcasted_iota(jnp.int32, grad_ref.shape, 1)

    def place_columns(i, x):
        shifted[i, :cols] = zero
        shifted[i, cols + pixels :] = zero
        shifted[i, cols : cols + pixels] = x.astype(jnp.bfloat16).reshape(pixels, chans)

    def tap_sum(b, total):
        for a in range(3):
            copies[3 * a + b].wait()
            total = total + dot(shifted[b, a * cols : a * cols + pixels], ups[3 * a + b], 1, 1)
        return total

    place_columns(1, grad_ref[...])
    total = tap_sum(1, 0.0)
    grad = grad_ref[...].astype(jnp.float32)
    place_columns(0, jnp.where(at == 0, low_ref[...].astype(jnp.float32), roll(grad, 1, 1)))
    total = tap_sum(0, total)
    place_columns(2, jnp.where(at == cols - 1, high_ref[...].astype(jnp.float32), roll(grad, -1, 1)))
    total = tap_sum(2, total)
    for c in range(0, pixels, CHUNK):
        pre = pre_ref[c : c + CHUNK].astype(jnp.float32)
        sigma = jax.nn.sigmoid(pre)
        slope = sigma * (1.0 + pre * (1.0 - sigma))
        feat[cols + c : cols + c + CHUNK] = (total[c : c + CHUNK] * slope).astype(jnp.bfloat16)
    part = sum(dot(feat[a * cols : a * cols + pixels], taps[2 - a], 1, 1) for a in range(3))
    part = part.reshape(rows, cols, 128)
    lane = lax.broadcasted_iota(jnp.int32, part.shape, 2)
    at = lax.broadcasted_iota(jnp.int32, part.shape, 1)
    after = jnp.where(lane < 16, part, 0.0)
    here = jnp.where(lane < 16, roll(part, -16, 2), 0.0)
    before = jnp.where(lane < 16, roll(part, -32, 2), 0.0)
    inner = (
        here
        + jnp.where(at == 0, 0.0, roll(before, 1, 1))
        + jnp.where(at == cols - 1, 0.0, roll(after, -1, 1))
    )
    edge = jnp.where(at == 0, roll(before, 1, 1), 0.0) + jnp.where(
        at == cols - 1, roll(after, -1, 1), 0.0
    )
    lat[...] = (inner + roll(edge, 64, 2)).reshape(pixels, 128)
    total = 0.0
    for b in range(2):
        pick = lat[pl.ds(b, pixels // 2, stride=2), :]
        pick = pick.reshape(rows // 2, 2, cols // 2, 128)
        for a in range(2):
            total = total + roll(pick[:, a], (2 * a + b) * 16, 2)
    out_ref[...] = total.reshape(pixels // 4, 128).astype(jnp.bfloat16)

    table = table_ref[...].astype(jnp.float32)
    at = lax.broadcasted_iota(jnp.int32, table.shape, 0)
    gate = jnp.sum(jnp.where(at == bucket[0], table, 0.0), axis=0, keepdims=True)
    gated = final_ref[...].astype(jnp.float32) * gate
    top = gated.astype(jnp.bfloat16)
    rest = (gated - top.astype(jnp.float32)).astype(jnp.bfloat16)
    copies[9].wait()
    mix = dot(part_ref[...], jnp.concatenate([top, rest], 0), 1, 1)
    mix = mix + roll(mix, 64, 1)
    top = mix.astype(jnp.bfloat16)
    rest = mix - top.astype(jnp.float32)
    lane = lax.broadcasted_iota(jnp.int32, mix.shape, 1)
    mix_ref[...] = jnp.where(lane < 64, mix, rest).astype(jnp.bfloat16)


def decoder(seat, bucket, grad, low, high, up_kernel, pre, in_kernel, table, final, weight, part):
    rows, cols, chans = grad.shape
    pixels = rows * cols
    taps = in_kernel.reshape(3, -1, chans)
    depth, width = final.shape
    whole = lambda *shape: pl.BlockSpec(shape, lambda t, s, b: (0,) * len(shape))
    return pl.pallas_call(
        conv_kernel,
        grid_spec=pltpu.PrefetchScalarGridSpec(
            num_scalar_prefetch=2,
            grid=(1,),
            in_specs=[
                whole(rows, cols, chans),
                whole(rows, 1, chans),
                whole(rows, 1, chans),
                pl.BlockSpec(memory_space=pl.ANY),
                whole(pixels, chans),
                whole(*taps.shape),
                whole(*table.shape),
                whole(depth, width),
                pl.BlockSpec(memory_space=pl.ANY),
            ],
            out_specs=[whole(pixels // 4, 128), whole(part, 2 * depth)],
            scratch_shapes=[
                pltpu.VMEM((3, pixels + 2 * cols, chans), jnp.bfloat16),
                pltpu.VMEM((pixels + 2 * cols, chans), jnp.bfloat16),
                pltpu.VMEM((3, 128, chans), jnp.bfloat16),
                pltpu.VMEM((pixels, 128), jnp.float32),
                pltpu.VMEM((9, chans, chans), jnp.bfloat16),
                pltpu.VMEM((part, width), jnp.bfloat16),
                pltpu.SemaphoreType.DMA((10,)),
            ],
        ),
        out_shape=[
            jax.ShapeDtypeStruct((pixels // 4, 128), jnp.bfloat16),
            jax.ShapeDtypeStruct((part, 2 * depth), jnp.bfloat16),
        ],
        compiler_params=pltpu.CompilerParams(vmem_limit_bytes=58 * 1024 * 1024),
        cost_estimate=pl.CostEstimate(
            flops=2 * 9 * pixels * chans * chans, bytes_accessed=9 * chans * chans * 2,
            transcendentals=pixels * chans,
        ),
        name="decoder",
    )(
        seat, bucket, grad, low, high, up_kernel, pre.reshape(pixels, chans), taps, table, final,
        weight,
    )


def turn_kernel(seat, rows_ref, kept_ref, given_ref):
    half = kept_ref.shape[0]
    low = seat[2]
    kept_ref[...] = rows_ref[:, pl.ds(pl.multiple_of(low * half, 128), half)].T
    given_ref[...] = rows_ref[:, pl.ds(pl.multiple_of((1 - low) * half, 128), half)].T


def turned(seat, rows):
    count, width = rows.shape
    whole = lambda *shape: pl.BlockSpec(shape, lambda i, s: (0,) * len(shape))
    return pl.pallas_call(
        turn_kernel,
        grid_spec=pltpu.PrefetchScalarGridSpec(
            num_scalar_prefetch=1,
            grid=(1,),
            in_specs=[whole(count, width)],
            out_specs=[whole(width // 2, count)] * 2,
        ),
        out_shape=[jax.ShapeDtypeStruct((width // 2, count), rows.dtype)] * 2,
        compiler_params=pltpu.CompilerParams(vmem_limit_bytes=8 * 1024 * 1024),
        cost_estimate=pl.CostEstimate(
            flops=0, bytes_accessed=4 * count * width, transcendentals=0
        ),
        name="turned",
    )(seat, rows)


def value_kernel(
    seat, q_ref, k_ref, *refs,
):
    pieces, (mix_ref, e_ref, g_ref, inv_ref, vg_ref, strips, patches) = refs[:8], refs[8:]
    head = pl.program_id(0)
    me = seat[0]

    @pl.when(head == 0)
    def _():
        strips[0] = jnp.zeros(strips.shape[1:], jnp.float32)
        strips[9] = jnp.zeros(strips.shape[1:], jnp.float32)
        for d, ref in enumerate(pieces):
            strips[(me ^ d) + 1] = ref[...].astype(jnp.float32)
        shape = (16, 8, 128)
        at = lax.broadcasted_iota(jnp.int32, shape, 1)
        lane = lax.broadcasted_iota(jnp.int32, shape, 2)
        for s in range(8):
            mine = strips[s + 1].reshape(shape)
            below = roll(strips[s].reshape(shape), 64, 2)
            above = roll(strips[s + 2].reshape(shape), 64, 2)
            joined = mine + jnp.where((at == 0) & (lane % 32 < 16), below, 0.0)
            joined = joined + jnp.where((at == 7) & (lane % 32 >= 16), above, 0.0)
            joined = jnp.where(lane < 64, joined, 0.0)
            patches[:, s * 8 : s * 8 + 8, :] = joined + roll(joined, 64, 2)

    scale = SCALE * math.log2(math.e)
    tokens = q_ref.shape[0]
    for c in range(0, tokens, SLAB):
        q = q_ref[c : c + SLAB]
        pat = patches[c // 64 : (c + SLAB) // 64].reshape(SLAB, 128).astype(jnp.bfloat16)
        grad_t = dot(mix_ref[...], pat, 1, 1)
        scores = dot(k_ref[...], q, 1, 1)
        top = jnp.max(scores, axis=0, keepdims=True)
        weights = jnp.exp2(scores * scale - top * scale)
        inverse = 1.0 / jnp.sum(weights, axis=0, keepdims=True)
        e_ref[0, :, c : c + SLAB] = weights.astype(jnp.bfloat16)
        g_ref[0, :, c : c + SLAB] = (grad_t * inverse).astype(jnp.bfloat16)
        inv_ref[0, :, c : c + SLAB] = inverse
    vg_ref[...] = dot(e_ref[0], g_ref[0], 1, 1).astype(jnp.bfloat16)


def value_part(qkv, strips, mix, me):
    tokens = qkv.shape[0]
    heads = qkv.shape[1] // (3 * DH)
    whole = lambda x: pl.BlockSpec(x.shape, lambda h, s: (0,) * x.ndim)
    return pl.pallas_call(
        value_kernel,
        grid_spec=pltpu.PrefetchScalarGridSpec(
            num_scalar_prefetch=1,
            grid=(heads,),
            in_specs=[
                pl.BlockSpec((tokens, DH), lambda h, s: (0, h)),
                pl.BlockSpec((tokens, DH), lambda h, s: (0, heads + h)),
                *[whole(x) for x in strips],
                pl.BlockSpec((DH, mix.shape[1]), lambda h, s: (h, 0)),
            ],
            out_specs=[
                pl.BlockSpec((1, tokens, tokens), lambda h, s: (h, 0, 0)),
                pl.BlockSpec((1, DH, tokens), lambda h, s: (h, 0, 0)),
                pl.BlockSpec((1, 1, tokens), lambda h, s: (h, 0, 0)),
                pl.BlockSpec((tokens, DH), lambda h, s: (0, h)),
            ],
            scratch_shapes=[
                pltpu.VMEM((10, 128, 128), jnp.float32),
                pltpu.VMEM((16, 64, 128), jnp.float32),
            ],
        ),
        out_shape=[
            jax.ShapeDtypeStruct((heads, tokens, tokens), jnp.bfloat16),
            jax.ShapeDtypeStruct((heads, DH, tokens), jnp.bfloat16),
            jax.ShapeDtypeStruct((heads, 1, tokens), jnp.float32),
            jax.ShapeDtypeStruct((tokens, heads * DH), jnp.bfloat16),
        ],
        compiler_params=pltpu.CompilerParams(vmem_limit_bytes=24 * 1024 * 1024),
        cost_estimate=pl.CostEstimate(
            flops=2 * 2 * heads * tokens * tokens * DH,
            bytes_accessed=heads * tokens * tokens * 2,
            transcendentals=heads * tokens * tokens,
        ),
        name="value_part",
    )(me, qkv, qkv, *strips, mix)


def score_kernel(q_ref, k_ref, v_ref, vg_ref, e_ref, g_ref, inv_ref, out_ref, kt_ref, ds_ref):
    head = pl.program_id(0)
    heads = pl.num_programs(0)
    tokens = q_ref.shape[0]
    kt_ref[...] = k_ref[...].T
    for c in range(0, tokens, PART):
        weights = e_ref[0, :, c : c + PART].astype(jnp.float32)
        prob_grad = dot(v_ref[...], g_ref[0, :, c : c + PART], 1, 0)
        row_dot = jnp.sum(weights * prob_grad, axis=0, keepdims=True) * inv_ref[0, :, c : c + PART]
        ds_ref[:, c : c + PART] = (weights * (prob_grad - row_dot)).astype(jnp.bfloat16)
    score_grad = ds_ref[...]
    at = pl.ds(pl.multiple_of(head * DH, DH), DH)
    out_ref[:, at] = (dot(kt_ref[...], score_grad, 1, 0).T * SCALE).astype(jnp.bfloat16)
    at = pl.ds(pl.multiple_of((heads + head) * DH, DH), DH)
    out_ref[:, at] = (dot(score_grad, q_ref[...], 1, 0) * SCALE).astype(jnp.bfloat16)
    at = pl.ds(pl.multiple_of((2 * heads + head) * DH, DH), DH)
    out_ref[:, at] = vg_ref[...]


def score_part(qkv, v_part, e, g, inv):
    tokens = qkv.shape[0]
    heads = qkv.shape[1] // (3 * DH)
    return pl.pallas_call(
        score_kernel,
        grid=(heads,),
        in_specs=[
            pl.BlockSpec((tokens, DH), lambda h: (0, h)),
            pl.BlockSpec((tokens, DH), lambda h: (0, heads + h)),
            pl.BlockSpec((tokens, DH), lambda h: (0, 2 * heads + h)),
            pl.BlockSpec((tokens, DH), lambda h: (0, h)),
            pl.BlockSpec((1, tokens, tokens), lambda h: (h, 0, 0)),
            pl.BlockSpec((1, DH, tokens), lambda h: (h, 0, 0)),
            pl.BlockSpec((1, 1, tokens), lambda h: (h, 0, 0)),
        ],
        out_specs=pl.BlockSpec((tokens, 3 * heads * DH), lambda h: (0, 0)),
        out_shape=jax.ShapeDtypeStruct((tokens, 3 * heads * DH), jnp.bfloat16),
        scratch_shapes=[
            pltpu.VMEM((DH, tokens), jnp.bfloat16),
            pltpu.VMEM((tokens, tokens), jnp.bfloat16),
        ],
        compiler_params=pltpu.CompilerParams(vmem_limit_bytes=24 * 1024 * 1024),
        cost_estimate=pl.CostEstimate(
            flops=3 * 2 * heads * tokens * tokens * DH,
            bytes_accessed=heads * tokens * tokens * 2,
            transcendentals=0,
        ),
        name="score_part",
    )(qkv, qkv, qkv, v_part, e, g, inv)


def weight_kernel(seat, *refs):
    pieces, (v_own, v_got, mine_ref, other_ref) = refs[:8], refs[8:]
    zed, low, core = seat[1], seat[2], seat[3]
    block = mine_ref.shape[1]
    ex = pl.program_id(0)
    for out_ref, side in ((mine_ref, core), (other_ref, 1 - core)):
        at = pl.ds(pl.multiple_of((2 * ex + side) * block, block), block)
        total = 0.0
        for i, d in enumerate((0, 3, 1, 2)):
            base = ((zed + d) % 4) * 256
            first = pl.ds(pl.multiple_of(base + low * 128, 128), 128)
            second = pl.ds(pl.multiple_of(base + (1 - low) * 128, 128), 128)
            rows = jnp.concatenate([pieces[2 * i][at], pieces[2 * i + 1][at]], 1)
            v = jnp.concatenate(
                [
                    jnp.concatenate([v_own[first], v_own[second]], 0),
                    jnp.concatenate([v_got[first], v_got[second]], 0),
                ],
                1,
            )
            total = total + dot(rows, v, 1, 0)
        out_ref[0] = total.astype(jnp.bfloat16)


def weight_part(pieces, v_own, v_got, seat):
    half, count = pieces[0].shape
    block = half // 8
    cols = 2 * v_own.shape[1]
    whole = lambda x: pl.BlockSpec(x.shape, lambda i, s: (0,) * x.ndim)
    return pl.pallas_call(
        weight_kernel,
        grid_spec=pltpu.PrefetchScalarGridSpec(
            num_scalar_prefetch=1,
            grid=(4,),
            in_specs=[whole(x) for x in (*pieces, v_own, v_got)],
            out_specs=[pl.BlockSpec((1, block, cols), lambda i, s: (i, 0, 0))] * 2,
        ),
        out_shape=[jax.ShapeDtypeStruct((4, block, cols), jnp.bfloat16)] * 2,
        compiler_params=pltpu.CompilerParams(vmem_limit_bytes=56 * 1024 * 1024),
        cost_estimate=pl.CostEstimate(
            flops=16 * count * half * cols, bytes_accessed=16 * count * half, transcendentals=0
        ),
        name="weight_part",
    )(seat, *pieces, v_own, v_got)


def merge_kernel(seat, mine_ref, came_ref, own_ref, *outs):
    ex = seat[4]

    def total(at):
        return mine_ref[at].astype(jnp.float32) + came_ref[at].astype(jnp.float32)

    own_ref[...] = total(ex)
    for d, out in enumerate(outs):
        out[...] = total(ex ^ (d + 1)).astype(jnp.bfloat16)


def merge(seat, mine, came):
    count, rows, cols = mine.shape
    whole = lambda *shape: pl.BlockSpec(shape, lambda i, s: (0,) * len(shape))
    return pl.pallas_call(
        merge_kernel,
        grid_spec=pltpu.PrefetchScalarGridSpec(
            num_scalar_prefetch=1,
            grid=(1,),
            in_specs=[whole(count, rows, cols)] * 2,
            out_specs=[whole(rows, cols)] * 4,
        ),
        out_shape=[jax.ShapeDtypeStruct((rows, cols), jnp.float32)]
        + [jax.ShapeDtypeStruct((rows, cols), jnp.bfloat16)] * 3,
        compiler_params=pltpu.CompilerParams(vmem_limit_bytes=8 * 1024 * 1024),
        cost_estimate=pl.CostEstimate(
            flops=count * rows * cols, bytes_accessed=6 * count * rows * cols, transcendentals=0
        ),
        name="merge",
    )(seat, mine, came)


def join_kernel(in_ref, *outs):
    cols = in_ref.shape[2] // 3
    for i, out in enumerate(outs):
        for j in range(in_ref.shape[0]):
            out[:, j * cols : (j + 1) * cols] = in_ref[j, :, i * cols : (i + 1) * cols]


def join(blocks):
    count, tokens, wide = blocks.shape
    cols = wide // 3
    out = jax.ShapeDtypeStruct((tokens, count * cols), blocks.dtype)
    return pl.pallas_call(
        join_kernel,
        grid=(4,),
        in_specs=[pl.BlockSpec((count // 4, tokens, wide), lambda i: (i, 0, 0))],
        out_specs=[pl.BlockSpec((tokens, count // 4 * cols), lambda i: (0, i))] * 3,
        out_shape=[out] * 3,
        cost_estimate=pl.CostEstimate(
            flops=0, bytes_accessed=4 * count * tokens * wide, transcendentals=0
        ),
        compiler_params=pltpu.CompilerParams(vmem_limit_bytes=8 * 1024 * 1024),
        name="join",
    )(blocks)


def place_kernel(seat, own, one, two, three, out_ref):
    zed, high = seat[1], seat[5]
    cols = own.shape[1] // 2
    for d, ref in enumerate((own, one, two, three)):
        source = (zed + 4 - d) % 4
        for h in range(2):
            at = pl.multiple_of((source * 2 + (high ^ h)) * cols, cols)
            out_ref[:, pl.ds(at, cols)] = ref[:, h * cols : (h + 1) * cols]


def place(parts, seat):
    rows, cols = parts[0].shape
    whole = pl.BlockSpec((rows, cols), lambda i, s: (0, 0))
    return pl.pallas_call(
        place_kernel,
        grid_spec=pltpu.PrefetchScalarGridSpec(
            num_scalar_prefetch=1,
            grid=(1,),
            in_specs=[whole] * 4,
            out_specs=pl.BlockSpec((rows, 4 * cols), lambda i, s: (0, 0)),
        ),
        out_shape=jax.ShapeDtypeStruct((rows, 4 * cols), jnp.float32),
        compiler_params=pltpu.CompilerParams(vmem_limit_bytes=8 * 1024 * 1024),
        name="place",
    )(seat, *parts)


def per_device(
    pre_activation,
    output_grad,
    up_kernel,
    in_kernel,
    final_weight,
    gate_table,
    bucket,
    query_vectors,
    key_vectors,
    value_vectors,
    out_weight,
    block_input,
):
    seq_size = lax.axis_size("seq")
    me_seq = lax.axis_index("seq")
    me_dp = lax.axis_index("dp")
    zed, low = me_seq >> 1, me_seq & 1
    core, ex, high = me_dp & 1, (me_dp >> 1) & 3, me_dp >> 3
    seats = jnp.stack([me_seq, zed, low, core, ex, high])
    output_grad, seats, scalars = lax.optimization_barrier(
        (
            output_grad,
            seats,
            (me_seq, zed, low, core, ex, high, low ^ 1, high ^ 1, ex ^ 1, ex ^ 2, ex ^ 3)
            + tuple((zed + d) & 3 for d in (1, 2, 3)),
        )
    )
    me_seq, zed, low, core, ex, high, _, high_far = scalars[:8]
    zed_far = scalars[11:]
    tokens, width = query_vectors.shape[1:]
    cols = width // seq_size

    def seq_move(x, target):
        return lax.ppermute(x, "seq", [(i, target(i)) for i in range(8)])

    def dp_move(x, target):
        return lax.ppermute(x, "dp", [(i, target(i)) for i in range(16)])

    grad = output_grad[0]
    forward = [(i, i + 1) for i in range(seq_size - 1)]
    backward = [(i + 1, i) for i in range(seq_size - 1)]
    from_low = lax.ppermute(grad[:, -1:], "seq", forward)
    from_high = lax.ppermute(grad[:, :1], "seq", backward)

    kept, given = turned(seats, block_input[0])
    got = seq_move(given, lambda i: i ^ 1)

    split = jnp.concatenate(
        [
            x[0].reshape(tokens, seq_size, cols)
            for x in (query_vectors, key_vectors, value_vectors)
        ],
        axis=2,
    ).transpose(1, 0, 2)
    qkv = lax.all_to_all(split, "seq", 0, 0, tiled=True)
    qkv = qkv.reshape(seq_size * tokens, 3 * cols)

    strip, mix = decoder(
        seats, bucket, grad, from_low, from_high, up_kernel, pre_activation[0], in_kernel,
        gate_table, final_weight, out_weight, cols,
    )
    strips = [strip] + [seq_move(strip, lambda i, d=d: i ^ d) for d in range(1, 8)]
    left_a = seq_move(kept, lambda i: (i + 2) % 8)
    right_b = seq_move(got, lambda i: (i - 2) % 8)
    left_b = seq_move(got, lambda i: (i + 2) % 8)
    right_a = seq_move(kept, lambda i: (i - 2) % 8)

    e, g, inv, v_part = value_part(qkv, strips, mix, seats)
    v_got = seq_move(v_part, lambda i: i ^ 1)
    far_a = seq_move(after(left_a, v_part), lambda i: (i + 2) % 8)
    far_b = seq_move(after(right_b, v_part), lambda i: (i - 2) % 8)
    grads = score_part(qkv, v_part, e, g, inv)
    blocks = lax.all_to_all(
        grads.reshape(seq_size, tokens, -1), "seq", 0, 0, tiled=True
    )

    pieces = (kept, got, left_a, left_b, right_a, right_b, far_a, far_b)
    v_got = after(v_got, grads)
    mine, other = weight_part(pieces, v_part, v_got, seats)
    came = dp_move(other, lambda i: i ^ 1)
    total, *sends = merge(seats, mine, came)
    for d in (2, 1, 3):
        total = total + dp_move(sends[d - 1], lambda i, d=d: i ^ (2 * d)).astype(jnp.float32)
    wide = total.shape[1]
    total = total.astype(jnp.bfloat16).reshape(4, 2, -1, wide)

    landed = 0.0
    for b in range(2):
        perm = []
        for dp in range(16):
            for s in range(8):
                yh, xc, z, yl = dp // 8, dp % 8, s // 2, s % 2
                perm.append((dp * 8 + s, (yl * 8 + xc) * 8 + z * 2 + (yh ^ b)))
        piece = lax.dynamic_index_in_dim(total, (high, high_far)[b], 1, False)
        landed = landed + lax.ppermute(piece, ("dp", "seq"), perm).astype(jnp.float32)
    landed = after(landed, blocks)
    parts = [lax.dynamic_index_in_dim(landed, zed, 0, False)]
    for d in (1, 2, 3):
        piece = lax.dynamic_index_in_dim(landed, zed_far[d - 1], 0, False)
        parts.append(seq_move(piece, lambda i, d=d: (i + 2 * d) % 8))
    weight_grad = place(parts, seats)

    query_grad, key_grad, value_grad = join(blocks)
    return (query_grad[None], key_grad[None], value_grad[None], weight_grad)


def solution(mesh):
    return jax.shard_map(
        per_device,
        mesh=mesh,
        in_specs=(
            P("dp", None, "seq", None),
            P("dp", None, "seq", None),
            P(),
            P(),
            P(),
            P(),
            P("dp"),
            P("dp", "seq", None),
            P("dp", "seq", None),
            P("dp", "seq", None),
            P(),
            P("dp", "seq", None),
        ),
        out_specs=(
            P("dp", "seq", None),
            P("dp", "seq", None),
            P("dp", "seq", None),
            P(("dp", "seq"), None),
        ),
        check_vma=False,
    )
```

```python
import math

import jax
import jax.numpy as jnp
from jax import lax
from jax.experimental import pallas as pl
from jax.experimental.pallas import tpu as pltpu
from jax.sharding import PartitionSpec as P


DH = 128
SCALE = DH ** (-0.5)
CHUNK = 512
PART = 512
SPLIT = 8
SLAB = 128


def dot(a, b, ca, cb):
    return lax.dot_general(a, b, (((ca,), (cb,)), ((), ())), preferred_element_type=jnp.float32)


def roll(x, shift, axis):
    return pltpu.roll(x, shift % x.shape[axis], axis)


def after(x, first):
    return lax.optimization_barrier((x, first))[0]


def conv_kernel(
    seat, bucket, grad_ref, low_ref, high_ref, up_ref, pre_ref, in_ref, table_ref, final_ref,
    weight_ref, out_ref, mix_ref, shifted, feat, taps, lat, ups, part_ref, sems,
):
    rows, cols, chans = grad_ref.shape
    pixels = rows * cols

    copies = [
        pltpu.make_async_copy(up_ref.at[2 - a, 2 - b], ups.at[3 * a + b], sems.at[3 * a + b])
        for a in range(3)
        for b in range(3)
    ]
    early = copies[1::3] + copies[0::3] + copies[2::3]
    count = part_ref.shape[0] // SPLIT
    for i in range(SPLIT):
        first = pl.multiple_of((seat[0] * SPLIT + i) * count, count)
        source = weight_ref.at[pl.ds(first, count)]
        target = part_ref.at[pl.ds(i * count, count)]
        copies.append(pltpu.make_async_copy(source, target, sems.at[9 + i]))
    for copy in early + copies[9:]:
        copy.start()
    zero = jnp.zeros((cols, chans), jnp.bfloat16)
    feat[:cols] = zero
    feat[cols + pixels :] = zero
    taps[...] = jnp.zeros_like(taps)
    taps[:, : in_ref.shape[1]] = in_ref[...]
    at = lax.broadcasted_iota(jnp.int32, grad_ref.shape, 1)

    def place_columns(i, x):
        shifted[i, :cols] = zero
        shifted[i, cols + pixels :] = zero
        shifted[i, cols : cols + pixels] = x.astype(jnp.bfloat16).reshape(pixels, chans)

    place_columns(1, grad_ref[...])
    grad = grad_ref[...].astype(jnp.float32)
    place_columns(0, jnp.where(at == 0, low_ref[...].astype(jnp.float32), roll(grad, 1, 1)))
    place_columns(2, jnp.where(at == cols - 1, high_ref[...].astype(jnp.float32), roll(grad, -1, 1)))
    total = 0.0
    for b in (1, 0, 2):
        if b != 2:
            for copy in copies[1:9:3] if b == 1 else copies[0:9:3] + copies[2:9:3] + copies[9:]:
                copy.wait()
        for a in range(3):
            total = total + dot(shifted[b, a * cols : a * cols + pixels], ups[3 * a + b], 1, 1)
    for c in range(0, pixels, CHUNK):
        pre = pre_ref[c : c + CHUNK].astype(jnp.float32)
        sigma = jax.nn.sigmoid(pre)
        slope = sigma * (1.0 + pre * (1.0 - sigma))
        feat[cols + c : cols + c + CHUNK] = (total[c : c + CHUNK] * slope).astype(jnp.bfloat16)
    part = sum(dot(feat[a * cols : a * cols + pixels], taps[2 - a], 1, 1) for a in range(3))
    part = part.reshape(rows, cols, 128)
    lane = lax.broadcasted_iota(jnp.int32, part.shape, 2)
    at = lax.broadcasted_iota(jnp.int32, part.shape, 1)
    after = jnp.where(lane < 16, part, 0.0)
    here = jnp.where(lane < 16, roll(part, -16, 2), 0.0)
    before = jnp.where(lane < 16, roll(part, -32, 2), 0.0)
    inner = (
        here
        + jnp.where(at == 0, 0.0, roll(before, 1, 1))
        + jnp.where(at == cols - 1, 0.0, roll(after, -1, 1))
    )
    edge = jnp.where(at == 0, roll(before, 1, 1), 0.0) + jnp.where(
        at == cols - 1, roll(after, -1, 1), 0.0
    )
    lat[...] = (inner + roll(edge, 64, 2)).reshape(pixels, 128)
    total = 0.0
    for b in range(2):
        pick = lat[pl.ds(b, pixels // 2, stride=2), :]
        pick = pick.reshape(rows // 2, 2, cols // 2, 128)
        for a in range(2):
            total = total + roll(pick[:, a], (2 * a + b) * 16, 2)
    out_ref[...] = total.reshape(pixels // 4, 128).astype(jnp.bfloat16)

    table = table_ref[...].astype(jnp.float32)
    at = lax.broadcasted_iota(jnp.int32, table.shape, 0)
    gate = jnp.sum(jnp.where(at == bucket[0], table, 0.0), axis=0, keepdims=True)
    gated = final_ref[...].astype(jnp.float32) * gate
    top = gated.astype(jnp.bfloat16)
    rest = (gated - top.astype(jnp.float32)).astype(jnp.bfloat16)
    mix = dot(part_ref[...], jnp.concatenate([top, rest], 0), 1, 1)
    mix = mix + roll(mix, 64, 1)
    top = mix.astype(jnp.bfloat16)
    rest = mix - top.astype(jnp.float32)
    lane = lax.broadcasted_iota(jnp.int32, mix.shape, 1)
    mix_ref[...] = jnp.where(lane < 64, mix, rest).astype(jnp.bfloat16)


def decoder(seat, bucket, grad, low, high, up_kernel, pre, in_kernel, table, final, weight, part):
    rows, cols, chans = grad.shape
    pixels = rows * cols
    taps = in_kernel.reshape(3, -1, chans)
    depth, width = final.shape
    whole = lambda *shape: pl.BlockSpec(shape, lambda t, s, b: (0,) * len(shape))
    return pl.pallas_call(
        conv_kernel,
        grid_spec=pltpu.PrefetchScalarGridSpec(
            num_scalar_prefetch=2,
            grid=(1,),
            in_specs=[
                whole(rows, cols, chans),
                whole(rows, 1, chans),
                whole(rows, 1, chans),
                pl.BlockSpec(memory_space=pl.ANY),
                whole(pixels, chans),
                whole(*taps.shape),
                whole(*table.shape),
                whole(depth, width),
                pl.BlockSpec(memory_space=pl.ANY),
            ],
            out_specs=[whole(pixels // 4, 128), whole(part, 2 * depth)],
            scratch_shapes=[
                pltpu.VMEM((3, pixels + 2 * cols, chans), jnp.bfloat16),
                pltpu.VMEM((pixels + 2 * cols, chans), jnp.bfloat16),
                pltpu.VMEM((3, 128, chans), jnp.bfloat16),
                pltpu.VMEM((pixels, 128), jnp.float32),
                pltpu.VMEM((9, chans, chans), jnp.bfloat16),
                pltpu.VMEM((part, width), jnp.bfloat16),
                pltpu.SemaphoreType.DMA((9 + SPLIT,)),
            ],
        ),
        out_shape=[
            jax.ShapeDtypeStruct((pixels // 4, 128), jnp.bfloat16),
            jax.ShapeDtypeStruct((part, 2 * depth), jnp.bfloat16),
        ],
        compiler_params=pltpu.CompilerParams(vmem_limit_bytes=58 * 1024 * 1024),
        cost_estimate=pl.CostEstimate(
            flops=2 * 9 * pixels * chans * chans, bytes_accessed=9 * chans * chans * 2,
            transcendentals=pixels * chans,
        ),
        name="decoder",
    )(
        seat, bucket, grad, low, high, up_kernel, pre.reshape(pixels, chans), taps, table, final,
        weight,
    )


def shuffle_kernel(seat, q_ref, k_ref, v_ref, kept_in, given_in, out_ref, kept_ref, given_ref):
    cols = out_ref.shape[2] // 3
    for i, ref in enumerate((q_ref, k_ref, v_ref)):
        for j in range(out_ref.shape[0]):
            out_ref[j, :, i * cols : (i + 1) * cols] = ref[:, j * cols : (j + 1) * cols]
    kept_ref[...] = kept_in[...].T
    given_ref[...] = given_in[...].T


def shuffled(seat, q, k, v, rows, parts):
    count, width = q.shape
    cols = width // parts
    piece = rows.shape[1] // 4
    steps = 2
    heads = pl.BlockSpec((count, width // steps), lambda i, s: (0, i))
    turned = pl.BlockSpec((piece, count), lambda i, s: (i, 0))
    return pl.pallas_call(
        shuffle_kernel,
        grid_spec=pltpu.PrefetchScalarGridSpec(
            num_scalar_prefetch=1,
            grid=(steps,),
            in_specs=[heads] * 3
            + [
                pl.BlockSpec((count, piece), lambda i, s: (0, 2 * s[0] + i)),
                pl.BlockSpec((count, piece), lambda i, s: (0, 2 * (1 - s[0]) + i)),
            ],
            out_specs=[
                pl.BlockSpec((parts // steps, count, 3 * cols), lambda i, s: (i, 0, 0)),
                turned,
                turned,
            ],
        ),
        out_shape=[jax.ShapeDtypeStruct((parts, count, 3 * cols), q.dtype)]
        + [jax.ShapeDtypeStruct((2 * piece, count), q.dtype)] * 2,
        compiler_params=pltpu.CompilerParams(vmem_limit_bytes=56 * 1024 * 1024),
        cost_estimate=pl.CostEstimate(
            flops=0, bytes_accessed=12 * count * width + 4 * count * rows.shape[1], transcendentals=0
        ),
        name="shuffled",
    )(seat, q, k, v, rows, rows)


def value_kernel(
    seat, q_ref, k_ref, *refs,
):
    pieces, (mix_ref, e_ref, g_ref, inv_ref, vg_ref, strips, patches) = refs[:2], refs[2:]
    head = pl.program_id(0)
    me = seat[0]

    @pl.when(head == 0)
    def _():
        strips[0] = jnp.zeros(strips.shape[1:], jnp.float32)
        strips[9] = jnp.zeros(strips.shape[1:], jnp.float32)
        for b, ref in enumerate(pieces):
            for d in range(4):
                strips[(me ^ b ^ (2 * d)) + 1] = ref[d].astype(jnp.float32)
        shape = (16, 8, 128)
        at = lax.broadcasted_iota(jnp.int32, shape, 1)
        lane = lax.broadcasted_iota(jnp.int32, shape, 2)
        for s in range(8):
            mine = strips[s + 1].reshape(shape)
            below = roll(strips[s].reshape(shape), 64, 2)
            above = roll(strips[s + 2].reshape(shape), 64, 2)
            joined = mine + jnp.where((at == 0) & (lane % 32 < 16), below, 0.0)
            joined = joined + jnp.where((at == 7) & (lane % 32 >= 16), above, 0.0)
            joined = jnp.where(lane < 64, joined, 0.0)
            patches[:, s * 8 : s * 8 + 8, :] = joined + roll(joined, 64, 2)

    scale = SCALE * math.log2(math.e)
    tokens = q_ref.shape[0]
    for c in range(0, tokens, SLAB):
        q = q_ref[c : c + SLAB]
        pat = patches[c // 64 : (c + SLAB) // 64].reshape(SLAB, 128).astype(jnp.bfloat16)
        grad_t = dot(mix_ref[...], pat, 1, 1)
        scores = dot(k_ref[...], q, 1, 1)
        top = jnp.max(scores, axis=0, keepdims=True)
        weights = jnp.exp2(scores * scale - top * scale)
        inverse = 1.0 / jnp.sum(weights, axis=0, keepdims=True)
        e_ref[0, :, c : c + SLAB] = weights.astype(jnp.bfloat16)
        g_ref[0, :, c : c + SLAB] = (grad_t * inverse).astype(jnp.bfloat16)
        inv_ref[0, :, c : c + SLAB] = inverse
    vg_ref[...] = dot(e_ref[0], g_ref[0], 1, 1).astype(jnp.bfloat16)


def value_part(qkv, strips, mix, me):
    tokens = qkv.shape[0]
    heads = qkv.shape[1] // (3 * DH)
    whole = lambda x: pl.BlockSpec(x.shape, lambda h, s: (0,) * x.ndim)
    return pl.pallas_call(
        value_kernel,
        grid_spec=pltpu.PrefetchScalarGridSpec(
            num_scalar_prefetch=1,
            grid=(heads,),
            in_specs=[
                pl.BlockSpec((tokens, DH), lambda h, s: (0, h)),
                pl.BlockSpec((tokens, DH), lambda h, s: (0, heads + h)),
                *[whole(x) for x in strips],
                pl.BlockSpec((DH, mix.shape[1]), lambda h, s: (h, 0)),
            ],
            out_specs=[
                pl.BlockSpec((1, tokens, tokens), lambda h, s: (h, 0, 0)),
                pl.BlockSpec((1, DH, tokens), lambda h, s: (h, 0, 0)),
                pl.BlockSpec((1, 1, tokens), lambda h, s: (h, 0, 0)),
                pl.BlockSpec((tokens, DH), lambda h, s: (0, h)),
            ],
            scratch_shapes=[
                pltpu.VMEM((10, 128, 128), jnp.float32),
                pltpu.VMEM((16, 64, 128), jnp.float32),
            ],
        ),
        out_shape=[
            jax.ShapeDtypeStruct((heads, tokens, tokens), jnp.bfloat16),
            jax.ShapeDtypeStruct((heads, DH, tokens), jnp.bfloat16),
            jax.ShapeDtypeStruct((heads, 1, tokens), jnp.float32),
            jax.ShapeDtypeStruct((tokens, heads * DH), jnp.bfloat16),
        ],
        compiler_params=pltpu.CompilerParams(vmem_limit_bytes=24 * 1024 * 1024),
        cost_estimate=pl.CostEstimate(
            flops=2 * 2 * heads * tokens * tokens * DH,
            bytes_accessed=heads * tokens * tokens * 2,
            transcendentals=heads * tokens * tokens,
        ),
        name="value_part",
    )(me, qkv, qkv, *strips, mix)


def score_kernel(q_ref, k_ref, v_ref, vg_ref, e_ref, g_ref, inv_ref, out_ref, kt_ref, ds_ref):
    head = pl.program_id(0)
    heads = pl.num_programs(0)
    tokens = q_ref.shape[0]
    kt_ref[...] = k_ref[...].T
    for c in range(0, tokens, PART):
        weights = e_ref[0, :, c : c + PART].astype(jnp.float32)
        prob_grad = dot(v_ref[...], g_ref[0, :, c : c + PART], 1, 0)
        row_dot = jnp.sum(weights * prob_grad, axis=0, keepdims=True) * inv_ref[0, :, c : c + PART]
        ds_ref[:, c : c + PART] = (weights * (prob_grad - row_dot)).astype(jnp.bfloat16)
    score_grad = ds_ref[...]
    at = pl.ds(pl.multiple_of(head * DH, DH), DH)
    out_ref[:, at] = (dot(kt_ref[...], score_grad, 1, 0).T * SCALE).astype(jnp.bfloat16)
    at = pl.ds(pl.multiple_of((heads + head) * DH, DH), DH)
    out_ref[:, at] = (dot(score_grad, q_ref[...], 1, 0) * SCALE).astype(jnp.bfloat16)
    at = pl.ds(pl.multiple_of((2 * heads + head) * DH, DH), DH)
    out_ref[:, at] = vg_ref[...]


def score_part(qkv, v_part, e, g, inv):
    tokens = qkv.shape[0]
    heads = qkv.shape[1] // (3 * DH)
    return pl.pallas_call(
        score_kernel,
        grid=(heads,),
        in_specs=[
            pl.BlockSpec((tokens, DH), lambda h: (0, h)),
            pl.BlockSpec((tokens, DH), lambda h: (0, heads + h)),
            pl.BlockSpec((tokens, DH), lambda h: (0, 2 * heads + h)),
            pl.BlockSpec((tokens, DH), lambda h: (0, h)),
            pl.BlockSpec((1, tokens, tokens), lambda h: (h, 0, 0)),
            pl.BlockSpec((1, DH, tokens), lambda h: (h, 0, 0)),
            pl.BlockSpec((1, 1, tokens), lambda h: (h, 0, 0)),
        ],
        out_specs=pl.BlockSpec((tokens, 3 * heads * DH), lambda h: (0, 0)),
        out_shape=jax.ShapeDtypeStruct((tokens, 3 * heads * DH), jnp.bfloat16),
        scratch_shapes=[
            pltpu.VMEM((DH, tokens), jnp.bfloat16),
            pltpu.VMEM((tokens, tokens), jnp.bfloat16),
        ],
        compiler_params=pltpu.CompilerParams(vmem_limit_bytes=24 * 1024 * 1024),
        cost_estimate=pl.CostEstimate(
            flops=3 * 2 * heads * tokens * tokens * DH,
            bytes_accessed=heads * tokens * tokens * 2,
            transcendentals=0,
        ),
        name="score_part",
    )(qkv, qkv, qkv, v_part, e, g, inv)


def weight_kernel(seat, *refs):
    pieces, (v_own, v_got, mine_ref, other_ref) = refs[:8], refs[8:]
    zed, low, core = seat[1], seat[2], seat[3]
    block = mine_ref.shape[1]
    ex = pl.program_id(0)
    for out_ref, side in ((mine_ref, core), (other_ref, 1 - core)):
        at = pl.ds(pl.multiple_of((2 * ex + side) * block, block), block)
        total = 0.0
        for i, d in enumerate((0, 3, 1, 2)):
            base = ((zed + d) % 4) * 256
            first = pl.ds(pl.multiple_of(base + low * 128, 128), 128)
            second = pl.ds(pl.multiple_of(base + (1 - low) * 128, 128), 128)
            rows = jnp.concatenate([pieces[2 * i][at], pieces[2 * i + 1][at]], 1)
            v = jnp.concatenate(
                [
                    jnp.concatenate([v_own[first], v_own[second]], 0),
                    jnp.concatenate([v_got[first], v_got[second]], 0),
                ],
                1,
            )
            total = total + dot(rows, v, 1, 0)
        out_ref[0] = total.astype(jnp.bfloat16)


def weight_part(pieces, v_own, v_got, seat):
    half, count = pieces[0].shape
    block = half // 8
    cols = 2 * v_own.shape[1]
    whole = lambda x: pl.BlockSpec(x.shape, lambda i, s: (0,) * x.ndim)
    return pl.pallas_call(
        weight_kernel,
        grid_spec=pltpu.PrefetchScalarGridSpec(
            num_scalar_prefetch=1,
            grid=(4,),
            in_specs=[whole(x) for x in (*pieces, v_own, v_got)],
            out_specs=[pl.BlockSpec((1, block, cols), lambda i, s: (i, 0, 0))] * 2,
        ),
        out_shape=[jax.ShapeDtypeStruct((4, block, cols), jnp.bfloat16)] * 2,
        compiler_params=pltpu.CompilerParams(vmem_limit_bytes=16 * 1024 * 1024),
        cost_estimate=pl.CostEstimate(
            flops=16 * count * half * cols, bytes_accessed=16 * count * half, transcendentals=0
        ),
        name="weight_part",
    )(seat, *pieces, v_own, v_got)


def merge_kernel(seat, mine_ref, came_ref, own_ref, *outs):
    ex = seat[4]

    def total(at):
        return mine_ref[at].astype(jnp.float32) + came_ref[at].astype(jnp.float32)

    own_ref[...] = total(ex)
    for d, out in enumerate(outs):
        out[...] = total(ex ^ (d + 1)).astype(jnp.bfloat16)


def merge(seat, mine, came):
    count, rows, cols = mine.shape
    whole = lambda *shape: pl.BlockSpec(shape, lambda i, s: (0,) * len(shape))
    return pl.pallas_call(
        merge_kernel,
        grid_spec=pltpu.PrefetchScalarGridSpec(
            num_scalar_prefetch=1,
            grid=(1,),
            in_specs=[whole(count, rows, cols)] * 2,
            out_specs=[whole(rows, cols)] * 4,
        ),
        out_shape=[jax.ShapeDtypeStruct((rows, cols), jnp.float32)]
        + [jax.ShapeDtypeStruct((rows, cols), jnp.bfloat16)] * 3,
        compiler_params=pltpu.CompilerParams(vmem_limit_bytes=8 * 1024 * 1024),
        cost_estimate=pl.CostEstimate(
            flops=count * rows * cols, bytes_accessed=6 * count * rows * cols, transcendentals=0
        ),
        name="merge",
    )(seat, mine, came)


def join_kernel(in_ref, *outs):
    cols = in_ref.shape[2] // 3
    for i, out in enumerate(outs):
        for j in range(in_ref.shape[0]):
            out[:, j * cols : (j + 1) * cols] = in_ref[j, :, i * cols : (i + 1) * cols]


def join(blocks):
    count, tokens, wide = blocks.shape
    cols = wide // 3
    out = jax.ShapeDtypeStruct((tokens, count * cols), blocks.dtype)
    return pl.pallas_call(
        join_kernel,
        grid=(4,),
        in_specs=[pl.BlockSpec((count // 4, tokens, wide), lambda i: (i, 0, 0))],
        out_specs=[pl.BlockSpec((tokens, count // 4 * cols), lambda i: (0, i))] * 3,
        out_shape=[out] * 3,
        cost_estimate=pl.CostEstimate(
            flops=0, bytes_accessed=4 * count * tokens * wide, transcendentals=0
        ),
        compiler_params=pltpu.CompilerParams(vmem_limit_bytes=8 * 1024 * 1024),
        name="join",
    )(blocks)


def place_kernel(seat, own, one, two, three, out_ref):
    zed, high = seat[1], seat[5]
    cols = own.shape[1] // 2
    for d, ref in enumerate((own, one, two, three)):
        source = (zed + 4 - d) % 4
        for h in range(2):
            at = pl.multiple_of((source * 2 + (high ^ h)) * cols, cols)
            out_ref[:, pl.ds(at, cols)] = ref[:, h * cols : (h + 1) * cols]


def place(parts, seat):
    rows, cols = parts[0].shape
    whole = pl.BlockSpec((rows, cols), lambda i, s: (0, 0))
    return pl.pallas_call(
        place_kernel,
        grid_spec=pltpu.PrefetchScalarGridSpec(
            num_scalar_prefetch=1,
            grid=(1,),
            in_specs=[whole] * 4,
            out_specs=pl.BlockSpec((rows, 4 * cols), lambda i, s: (0, 0)),
        ),
        out_shape=jax.ShapeDtypeStruct((rows, 4 * cols), jnp.float32),
        compiler_params=pltpu.CompilerParams(vmem_limit_bytes=8 * 1024 * 1024),
        name="place",
    )(seat, *parts)


def per_device(
    pre_activation,
    output_grad,
    up_kernel,
    in_kernel,
    final_weight,
    gate_table,
    bucket,
    query_vectors,
    key_vectors,
    value_vectors,
    out_weight,
    block_input,
):
    seq_size = lax.axis_size("seq")
    me_seq = lax.axis_index("seq")
    me_dp = lax.axis_index("dp")
    zed, low = me_seq >> 1, me_seq & 1
    core, ex, high = me_dp & 1, (me_dp >> 1) & 3, me_dp >> 3
    output_grad, scalars = lax.optimization_barrier(
        (
            output_grad,
            (me_seq, zed, low, core, ex, high, low ^ 1, high ^ 1, ex ^ 1, ex ^ 2, ex ^ 3)
            + tuple((zed + d) & 3 for d in (1, 2, 3)),
        )
    )
    me_seq, zed, low, core, ex, high, _, high_far = scalars[:8]
    zed_far = scalars[11:]
    seats = jnp.stack([me_seq, zed, low, core, ex, high])
    tokens, width = query_vectors.shape[1:]
    cols = width // seq_size

    def seq_move(x, target):
        return lax.ppermute(x, "seq", [(i, target(i)) for i in range(8)])

    def dp_move(x, target):
        return lax.ppermute(x, "dp", [(i, target(i)) for i in range(16)])

    grad = output_grad[0]
    forward = [(i, i + 1) for i in range(seq_size - 1)]
    backward = [(i + 1, i) for i in range(seq_size - 1)]
    from_low = lax.ppermute(grad[:, -1:], "seq", forward)
    from_high = lax.ppermute(grad[:, :1], "seq", backward)

    split, kept, given = shuffled(
        low[None], query_vectors[0], key_vectors[0], value_vectors[0], block_input[0], seq_size
    )
    got = seq_move(given, lambda i: i ^ 1)

    qkv = lax.all_to_all(split, "seq", 0, 0, tiled=True)
    qkv = qkv.reshape(seq_size * tokens, 3 * cols)

    strip, mix = decoder(
        seats, bucket, grad, from_low, from_high, up_kernel, pre_activation[0], in_kernel,
        gate_table, final_weight, out_weight, cols,
    )
    near, last = (seq_move(strip, lambda i, d=d: i ^ d) for d in (2, 6))
    far = seq_move(strip, lambda i: i ^ 4)
    quad = jnp.stack([strip, near, far, last])
    kept_now = after(kept, strip)
    left_a = seq_move(kept_now, lambda i: (i + 2) % 8)
    right_a = seq_move(kept_now, lambda i: (i - 2) % 8)
    strips = (quad, seq_move(quad, lambda i: i ^ 1))
    right_b = seq_move(got, lambda i: (i - 2) % 8)
    left_b = seq_move(got, lambda i: (i + 2) % 8)

    e, g, inv, v_part = value_part(qkv, strips, mix, seats)
    v_got = seq_move(v_part, lambda i: i ^ 1)
    far_a = seq_move(after(left_a, v_part), lambda i: (i + 2) % 8)
    far_b = seq_move(after(right_b, v_part), lambda i: (i - 2) % 8)
    grads = score_part(qkv, v_part, e, g, inv)
    blocks = lax.all_to_all(
        grads.reshape(seq_size, tokens, -1), "seq", 0, 0, tiled=True
    )

    pieces = (kept, got, left_a, left_b, right_a, right_b, far_a, far_b)
    v_got = after(v_got, grads)
    mine, other = weight_part(pieces, v_part, v_got, seats)
    came = dp_move(other, lambda i: i ^ 1)
    total, *sends = merge(seats, mine, came)
    for d in (2, 1, 3):
        total = total + dp_move(sends[d - 1], lambda i, d=d: i ^ (2 * d)).astype(jnp.float32)
    wide = total.shape[1]
    total = total.astype(jnp.bfloat16).reshape(4, 2, -1, wide)

    arrived = []
    for b in range(2):
        perm = []
        for dp in range(16):
            for q in range(8):
                yh, xc, z, yl = dp // 8, dp % 8, q // 2, q % 2
                perm.append((dp * 8 + q, (yl * 8 + xc) * 8 + z * 2 + (yh ^ b)))
        piece = lax.dynamic_index_in_dim(total, (high, high_far)[b], 1, False)
        arrived.append(lax.ppermute(piece, ("dp", "seq"), perm))
    landed = arrived[0].astype(jnp.float32) + arrived[1].astype(jnp.float32)
    landed = after(landed, blocks)
    parts = [lax.dynamic_index_in_dim(landed, zed, 0, False)]
    for d in (1, 2, 3):
        piece = lax.dynamic_index_in_dim(landed, zed_far[d - 1], 0, False)
        parts.append(seq_move(piece, lambda i, d=d: (i + 2 * d) % 8))
    weight_grad = place(parts, seats)

    query_grad, key_grad, value_grad = join(blocks)
    return (query_grad[None], key_grad[None], value_grad[None], weight_grad)


def solution(mesh):
    return jax.shard_map(
        per_device,
        mesh=mesh,
        in_specs=(
            P("dp", None, "seq", None),
            P("dp", None, "seq", None),
            P(),
            P(),
            P(),
            P(),
            P("dp"),
            P("dp", "seq", None),
            P("dp", "seq", None),
            P("dp", "seq", None),
            P(),
            P("dp", "seq", None),
        ),
        out_specs=(
            P("dp", "seq", None),
            P("dp", "seq", None),
            P("dp", "seq", None),
            P(("dp", "seq"), None),
        ),
        check_vma=False,
    )
```
